256 devices in a mesh: member: 32 (over x, y, core), grid: 8 (over z).
Axes of the slice: x: 4, y: 4, z: 8, core: 2. Of those that a mesh axis runs over, the one named last changes fastest.
Arguments:
- prior_ensemble: bfloat16 [512, 48, 32768], P('member', None, 'grid'), may hold values from -6 to 6
- measured_location: int32 [8, 32, 128], P('grid', 'member'), may hold values from 0 to 6143
- measured_tally: int32 [8, 32], P('grid', 'member'), may hold values from 32 to 128, as said below
- measured_reading: float32 [8, 32, 128], P('grid', 'member'), may hold values from -6 to 6
- measured_noise_sigma: float32 [8, 32, 128], P('grid', 'member'), may hold values from 0.5 to 20, as said below
Outputs:
- analysis: bfloat16 [512, 48, 32768], P('member', None, 'grid')
The draws below stay inside these ranges and needn't reach their ends.
Inputs may be any that keep to these rules, and one draw needn't show every extreme that they name: `measured_location`: cell of the observation within its block of 48 rows and 128 columns. `measured_tally`: some block in every draw uses all 128 slots. `measured_noise_sigma`: positive error deviations.
All inputs are finite; a program needn't handle non-finite values.
Results may differ from the reference program's by a relative error of at most 0.0058.
Values may be sent and summed in bfloat16 or wider, within the bound.
A program may use at most 128 MiB of HBM per device.

```python
import jax
import jax.numpy as jnp
from jax import lax

ENSEMBLE_SIZE = 512
SHARD_WIDTH = 128
PROFILE_LENGTH = 48
OBS_SUB = 128
GRID_TILES = 8
SUB_TILES = 32
MESH_WIDTH = 32768


def draw_measured_tally(key, part):
    counts = jax.random.randint(key, (GRID_TILES, SUB_TILES), OBS_SUB // 4, OBS_SUB + 1)
    chosen = jax.random.randint(jax.random.fold_in(key, 7), (), 0, GRID_TILES * SUB_TILES)
    flat_index = jnp.arange(GRID_TILES * SUB_TILES).reshape(GRID_TILES, SUB_TILES)
    return jnp.where(flat_index == chosen, OBS_SUB, counts).astype(jnp.int32)


def draw_measured_noise_sigma(key, part):
    tile_count = GRID_TILES * SUB_TILES
    grid_pos = jnp.arange(GRID_TILES, dtype=jnp.float32)[:, None, None]
    member_pos = jnp.arange(SUB_TILES, dtype=jnp.float32)[None, :, None]
    ranked = (member_pos * GRID_TILES + grid_pos) / max(tile_count - 1, 1)
    spread_base = jnp.exp(jax.random.uniform(key, (GRID_TILES, SUB_TILES, OBS_SUB), jnp.float32, jnp.log(2.0), jnp.log(20.0)))
    return spread_base * jnp.exp(-0.5 * jnp.log(3.0) * ranked)


def touch_ends(values, own_key, smallest, high):
    longest = values.shape.index(max(values.shape))
    spots = []
    for shift in (0, 1):
        where = [jax.random.randint(jax.random.fold_in(own_key, axis), (), 0, length) for axis, length in enumerate(values.shape)]
        where[longest] = (where[longest] + shift) % values.shape[longest]
        spots.append(tuple(where))
    return values.at[spots[0]].set(smallest).at[spots[1]].set(high)


def block_levels(rng, shape, pieces, least, largest):
    def one(dim, blocks):
        draws = jax.random.uniform(jax.random.fold_in(jax.random.fold_in(rng, 6), dim), (blocks,), jnp.float32, least / len(pieces), largest / len(pieces))
        return jnp.repeat(jnp.exp(draws), shape[dim] // blocks).reshape((-1,) + (1,) * (len(shape) - dim - 1))

    factor_of = one(*pieces[0])
    for cut in pieces[1:]:
        factor_of = factor_of * one(*cut)
    return factor_of


def scatter_about(stream_key, dims, scale, most, pieces=(), kind=jnp.bfloat16):
    gain = block_levels(stream_key, dims, pieces, -0.22, 0.18) if pieces else 1.0
    entries = jax.random.normal(stream_key, dims, jnp.float32) * scale * gain
    return jnp.minimum(jnp.maximum(entries, -most), most).astype(kind)


def setup_inputs(seed: int = 0) -> dict:
    key_list = jax.random.split(jax.random.key(seed), 6)
    prior_ensemble = scatter_about(key_list[0], (ENSEMBLE_SIZE, PROFILE_LENGTH, MESH_WIDTH), 1.0, 6.0, ((0, 32), (2, 8)))
    measured_location = touch_ends(jax.random.randint(key_list[1], (GRID_TILES, SUB_TILES, OBS_SUB), 0, PROFILE_LENGTH * SHARD_WIDTH), jax.random.fold_in(key_list[1], 1), 0, (PROFILE_LENGTH * SHARD_WIDTH) - 1).astype(jnp.int32)
    measured_tally = draw_measured_tally(jax.random.fold_in(key_list[5], 71), 0)
    measured_reading = scatter_about(key_list[3], (GRID_TILES, SUB_TILES, OBS_SUB), 1.0, 6.0, ((0, 8), (1, 32)), jnp.float32)
    measured_noise_sigma = draw_measured_noise_sigma(jax.random.fold_in(key_list[5], 71), 0)
    return {"prior_ensemble": prior_ensemble, "measured_location": measured_location, "measured_tally": measured_tally, "measured_reading": measured_reading, "measured_noise_sigma": measured_noise_sigma}


HIGHEST_PRECISION = lax.Precision.HIGHEST

def whiten(hx_values, values, errors, obs_total):
    hx_float = hx_values.astype(jnp.float32)
    hx_mean = lax.optimization_barrier(jnp.mean(hx_float, axis=0))
    usable = (jnp.arange(hx_values.shape[1], dtype=jnp.int32) < obs_total).astype(jnp.float32)
    scale_obs = usable / errors
    whitened = (hx_float - hx_mean) * scale_obs
    innovation = (values - hx_mean) * scale_obs
    return (whitened, innovation)

def transform_matrix(gram_total, drive_vector):
    members = gram_total.shape[0]
    identity = jnp.eye(members, dtype=jnp.float32)
    system = (members - 1.0) * identity + gram_total
    factor_low = jnp.linalg.cholesky(system)
    inverse = jax.scipy.linalg.solve_triangular(factor_low, identity, lower=True)
    inner = jnp.dot(inverse, drive_vector, precision=HIGHEST_PRECISION)
    mean_weight = jnp.dot(inverse.T, inner, precision=HIGHEST_PRECISION)
    spread = jnp.sqrt(members - 1.0) * inverse.T
    return (mean_weight[:, None] + spread).astype(jnp.bfloat16)

def apply_block(state_block, transform):
    members, row_count, columns = state_block.shape
    flattened = state_block.reshape(members, row_count * columns)
    state_mean = lax.optimization_barrier(jnp.mean(flattened.astype(jnp.float32), axis=0))
    anomalies = (flattened.astype(jnp.float32) - state_mean).astype(jnp.bfloat16)
    increment = lax.dot_general(transform.astype(jnp.float32), anomalies.astype(jnp.float32), (((0,), (0,)), ((), ())), preferred_element_type=jnp.float32)
    return (state_mean + increment).astype(jnp.bfloat16).reshape(members, row_count, columns)

def reference(prior_ensemble, measured_location, measured_tally, measured_reading, measured_noise_sigma):
    patch_number = GRID_TILES * SUB_TILES
    cell_table = measured_location.reshape(patch_number, OBS_SUB)
    count_table = measured_tally.reshape(patch_number)
    value_table = measured_reading.reshape(patch_number, OBS_SUB)
    error_table = measured_noise_sigma.reshape(patch_number, OBS_SUB)

    def state_tile(tile_index):
        leading_shift = (tile_index * SHARD_WIDTH).astype(jnp.int32)
        return lax.dynamic_slice_in_dim(prior_ensemble, leading_shift, SHARD_WIDTH, 2)

    def accumulate(carry, tile_index):
        gram_total, drive_vector = carry
        state_block = state_tile(tile_index).reshape(ENSEMBLE_SIZE, PROFILE_LENGTH * SHARD_WIDTH)
        hx_values = jnp.take(state_block, cell_table[tile_index], axis=1)
        whitened, innovation = whiten(hx_values, value_table[tile_index], error_table[tile_index], count_table[tile_index])
        gram_total = gram_total + lax.dot_general(whitened, whitened, (((1,), (1,)), ((), ())), precision=HIGHEST_PRECISION)
        drive_vector = drive_vector + jnp.dot(whitened, innovation, precision=HIGHEST_PRECISION)
        return ((gram_total, drive_vector), tile_index)
    start_carry = (jnp.zeros((ENSEMBLE_SIZE, ENSEMBLE_SIZE), jnp.float32), jnp.zeros((ENSEMBLE_SIZE,), jnp.float32))
    (gram_total, drive_vector), unused = lax.scan(accumulate, start_carry, jnp.arange(patch_number, dtype=jnp.int32))
    transform = transform_matrix(gram_total, drive_vector)

    def correct_patch_field(tile_index, analysis):
        updated = apply_block(state_tile(tile_index), transform)
        leading_shift = (tile_index * SHARD_WIDTH).astype(jnp.int32)
        return lax.dynamic_update_slice_in_dim(analysis, updated, leading_shift, 2)
    return lax.fori_loop(0, patch_number, correct_patch_field, jnp.zeros_like(prior_ensemble))
```

```python
import functools

import jax
import jax.numpy as jnp
from jax import lax
from jax.experimental import pallas as pl
from jax.experimental.pallas import tpu as pltpu
from jax.sharding import PartitionSpec as P

HIGHEST = lax.Precision.HIGHEST
MESH = pl.DeviceIdType.MESH
ANY = pl.ANY

N = 512
G = 32
B = N // G
Z = 8
R = 48
C = 128
OBS = 128
EXT = N + 128
SLAB = 8
SLABS = R // SLAB

ORDER = (8, 24, 16, 2, 6, 4, 1, 9, 25, 17, 3, 7, 5, 10, 26, 18, 11, 27, 19, 12, 28, 20, 13, 29, 21, 14, 30, 22, 15, 31, 23)


def peer_of(me, r):
    dx, dy, dc = r // 8, (r // 2) % 4, r % 2
    x, y, c = me // 8, (me // 2) % 4, me % 2
    s = 1 - 2 * c
    return ((x + s * dx + 4) % 4) * 8 + ((y + s * dy + 4) % 4) * 2 + (c + dc) % 2


def at_member(p):
    return {"member": p}


def at_grid(q):
    return {"grid": q}


def gather_kernel(bulk_at, prior, loc, val, scale, X, gram, pv, locs, hxs, hxr, gl, rs, part, zr, total,
                  local_sem, bulk_s, bulk_r, loc_s, loc_r, hx_s, hx_r, rs_s, rs_r, z_s, z_r, ag_s, ag_r):
    me = lax.axis_index("member")
    g = lax.axis_index("grid")
    row = pl.multiple_of(me * B, B)

    def bulk(r):
        p = peer_of(me, r)
        return pltpu.make_async_remote_copy(
            src_ref=prior.at[:, :, pl.ds(pl.multiple_of(p * C, C), C)], dst_ref=X.at[pl.ds(row, B)],
            send_sem=bulk_s.at[r], recv_sem=bulk_r.at[r], device_id=at_member(p), device_id_type=MESH)

    def send_bulk(stage):
        for r in ORDER[bulk_at[stage]:bulk_at[stage + 1]]:
            bulk(r).start()

    def plane(src, dst, s, t, r):
        p = peer_of(me, r)
        return pltpu.make_async_remote_copy(
            src_ref=src(p), dst_ref=dst, send_sem=s.at[r], recv_sem=t.at[r],
            device_id=at_member(p), device_id_type=MESH)

    load = pltpu.make_async_copy(prior, pv, local_sem.at[0])
    load.start()

    bar = pltpu.get_barrier_semaphore()

    @pl.loop(1, G)
    def _(r):
        pl.semaphore_signal(bar, inc=1, device_id=at_member(peer_of(me, r)), device_id_type=MESH)

    @pl.loop(1, Z)
    def _(d):
        pl.semaphore_signal(bar, inc=1, device_id=at_grid((g + d) % Z), device_id_type=MESH)

    pl.semaphore_wait(bar, G - 1 + Z - 1)

    def loc_copy(r):
        return plane(lambda p: loc, locs.at[me], loc_s, loc_r, r)

    @pl.loop(1, G)
    def _(r):
        loc_copy(r).start()

    locs[me] = loc[...]
    send_bulk(0)
    load.wait()
    own = pltpu.make_async_copy(pv.at[:, :, pl.ds(pl.multiple_of(me * C, C), C)], X.at[pl.ds(row, B)], local_sem.at[1])
    own.start()

    @pl.loop(1, G)
    def _(r):
        loc_copy(r).wait()

    def hx_copy(r):
        return plane(lambda p: hxs.at[p], hxr.at[pl.ds(row, B)], hx_s, hx_r, r)

    def observe(b):
        cell = locs[b]
        lane = cell % C
        level = cell // C
        pick = (lax.broadcasted_iota(jnp.int32, (C, OBS), 0) == lane).astype(jnp.bfloat16)
        keep = lax.broadcasted_iota(jnp.int32, (R, OBS), 0) == level
        block = pv[:, :, pl.ds(pl.multiple_of(b * C, C), C)].reshape(B * R, C)
        both = jnp.dot(block, pick, preferred_element_type=jnp.float32).reshape(B, R, OBS)
        return jnp.sum(jnp.where(keep[None], both, 0.0), axis=1).astype(jnp.bfloat16)

    @pl.loop(1, G + 1)
    def _(r):
        @pl.when(r < G)
        def _():
            p = peer_of(me, r)
            hxs[p] = observe(p)

        @pl.when(r > 1)
        def _():
            hx_copy(r - 1).start()

    hxr[pl.ds(row, B), :] = observe(me)
    send_bulk(1)

    @pl.loop(1, G)
    def _(r):
        hx_copy(r).wait()

    hx = hxr[...].astype(jnp.float32)
    mean = jnp.sum(hx, axis=0, keepdims=True) * (1.0 / N)
    white = (hx - mean) * scale[...]
    innovation = (val[...] - mean) * scale[...]
    first = lax.broadcasted_iota(jnp.int32, (128, OBS), 0) == 0
    side = jnp.where(first, innovation, 0.0)
    last = (((1,), (1,)), ((), ()))
    for i in range(4):
        rows = pl.ds(i * 128, 128)
        w_i = white[i * 128:(i + 1) * 128]
        gl[rows, :N] = lax.dot_general(w_i, white, last, precision=HIGHEST, preferred_element_type=jnp.float32)
        gl[rows, N:] = lax.dot_general(w_i, side, last, precision=HIGHEST, preferred_element_type=jnp.float32)

    def rs_copy(r):
        return plane(lambda p: gl.at[pl.ds(pl.multiple_of(p * B, B), B)], rs.at[me], rs_s, rs_r, r)

    @pl.loop(1, G)
    def _(r):
        rs_copy(r).start()

    rs[me] = gl[pl.ds(row, B), :]
    send_bulk(2)

    @pl.loop(1, G)
    def _(r):
        rs_copy(r).wait()

    part[...] = lax.fori_loop(1, G, lambda i, t: t + rs[i], rs[0])

    def z_copy(d):
        return pltpu.make_async_remote_copy(
            src_ref=part, dst_ref=zr.at[g], send_sem=z_s.at[d], recv_sem=z_r.at[d],
            device_id=at_grid((g + d) % Z), device_id_type=MESH)

    zr[g] = part[...]

    @pl.loop(1, Z)
    def _(d):
        z_copy(d).start()

    send_bulk(3)

    @pl.loop(1, Z)
    def _(d):
        z_copy(d).wait()

    total[...] = lax.fori_loop(1, Z, lambda i, t: t + zr[i], zr[0])

    def ag_copy(r):
        return plane(lambda p: total, gram.at[pl.ds(row, B)], ag_s, ag_r, r)

    gram[pl.ds(row, B), :] = total[...]

    @pl.loop(1, G)
    def _(r):
        ag_copy(r).start()

    send_bulk(4)

    @pl.loop(1, G)
    def _(r):
        ag_copy(r).wait()

    own.wait()

    @pl.loop(1, G)
    def _(r):
        bulk(r).wait()


def gather_and_sum(prior, loc, val, scale, bulk_at):
    vmem = pl.BlockSpec(memory_space=pltpu.VMEM)
    anym = pl.BlockSpec(memory_space=ANY)
    dma = pltpu.SemaphoreType.DMA
    return pl.pallas_call(
        functools.partial(gather_kernel, bulk_at),
        out_shape=(jax.ShapeDtypeStruct((N, R, C), jnp.bfloat16), jax.ShapeDtypeStruct((N, EXT), jnp.float32)),
        in_specs=[anym, vmem, vmem, vmem],
        out_specs=(anym, vmem),
        scratch_shapes=[
            pltpu.VMEM((B, R, G * C), jnp.bfloat16),
            pltpu.VMEM((G, 1, OBS), jnp.int32),
            pltpu.VMEM((G, B, OBS), jnp.bfloat16),
            pltpu.VMEM((N, OBS), jnp.bfloat16),
            pltpu.VMEM((N, EXT), jnp.float32),
            pltpu.VMEM((G, B, EXT), jnp.float32),
            pltpu.VMEM((B, EXT), jnp.float32),
            pltpu.VMEM((Z, B, EXT), jnp.float32),
            pltpu.VMEM((B, EXT), jnp.float32),
            dma((2,)), dma((G,)), dma((G,)), dma((G,)), dma((G,)), dma((G,)), dma((G,)),
            dma((G,)), dma((G,)), dma((Z,)), dma((Z,)), dma((G,)), dma((G,)),
        ],
        compiler_params=pltpu.CompilerParams(collective_id=0, has_side_effects=True, vmem_limit_bytes=48 << 20),
        name="gather_and_sum",
    )(prior, loc, val, scale)


LOOSE = 0.15
TIGHT = 1e-7


def factor_kernel(gram, out, a, m, b):
    eye = (lax.broadcasted_iota(jnp.int32, (N, N), 0) == lax.broadcasted_iota(jnp.int32, (N, N), 1)).astype(jnp.float32)
    a[...] = gram[:, :N] + (N - 1.0) * eye
    diagonal = jnp.sum(a[...] * eye, axis=1, keepdims=True)
    m[...] = eye * lax.rsqrt(diagonal)
    rhs_t = (((1,), (1,)), ((), ()))

    def update(precision):
        t = jnp.dot(m[...], a[...], precision=precision, preferred_element_type=jnp.float32)
        e = lax.dot_general(t, m[...], rhs_t, precision=precision, preferred_element_type=jnp.float32)
        rows = lax.broadcasted_iota(jnp.int32, (N, N), 0)
        cols = lax.broadcasted_iota(jnp.int32, (N, N), 1)
        same = rows == cols
        e = jnp.where(same, e - 1.0, e)
        low = jnp.where(cols < rows, e, jnp.where(same, 0.5 * e, 0.0))
        m[...] -= jnp.dot(low, m[...], precision=precision, preferred_element_type=jnp.float32)
        return 2.0 * jnp.sum(low * low)

    def steps(precision, bound, most, start):
        return lax.while_loop(
            lambda s: (s[0] < most) & (s[1] > bound),
            lambda s: (s[0] + 1, update(precision)), (0, start))[1]

    left = steps(lax.Precision.DEFAULT, LOOSE, 16, jnp.float32(1e30))
    left = steps(HIGHEST, TIGHT, 8, jnp.float32(1e30))

    @pl.when(jnp.logical_not(left <= TIGHT))
    def _():
        a[...] = gram[:, :N] + (N - 1.0) * eye
        m[...] = eye

        @pl.loop(0, N)
        def _(k):
            pivot_row = a[pl.ds(k, 1), :]
            lanes = lax.broadcasted_iota(jnp.int32, (1, N), 1)
            pivot = jnp.sum(jnp.where(lanes == k, pivot_row, 0.0), axis=1, keepdims=True)
            inv = 1.0 / jnp.sqrt(pivot)
            u = pivot_row * inv
            v = m[pl.ds(k, 1), :] * inv
            m[pl.ds(k, 1), :] = v

            @pl.loop(0, N // 64)
            def _(i):
                rows = pl.ds(pl.multiple_of(i * 64, 64), 64)
                blk = a[rows, :]
                cols = lax.broadcasted_iota(jnp.int32, (64, N), 1)
                ids = lax.broadcasted_iota(jnp.int32, (64, 1), 0) + i * 64
                col = jnp.sum(jnp.where(cols == k, blk, 0.0), axis=1, keepdims=True) * inv
                col = jnp.where(ids > k, col, 0.0)
                a[rows, :] = blk - col * u
                m[rows, :] = m[rows, :] - col * v

    drive = gram[:, N:]
    inner = jnp.dot(m[...], drive, precision=HIGHEST, preferred_element_type=jnp.float32)
    weight = lax.dot_general(inner, m[...], (((0,), (0,)), ((), ())), precision=HIGHEST,
                             preferred_element_type=jnp.float32)[0:1]
    out[...] = (weight + jnp.sqrt(jnp.float32(N - 1.0)) * m[...]).astype(jnp.bfloat16)


def transform_rows(gram):
    vmem = pl.BlockSpec(memory_space=pltpu.VMEM)
    return pl.pallas_call(
        factor_kernel,
        out_shape=jax.ShapeDtypeStruct((N, N), jnp.bfloat16),
        in_specs=[vmem], out_specs=vmem,
        scratch_shapes=[pltpu.VMEM((N, N), jnp.float32)] * 3,
        compiler_params=pltpu.CompilerParams(vmem_limit_bytes=48 << 20),
        name="transform_rows",
    )(gram)


def apply_kernel(X, tt, out, xin, xf, of, ob, load_sem, own_sem, send_s, recv_s):
    me = lax.axis_index("member")

    def load(s):
        return pltpu.make_async_copy(X.at[:, pl.ds(s * SLAB, SLAB), :], xin.at[s], load_sem.at[s])

    for s in range(SLABS):
        load(s).start()

    bar = pltpu.get_barrier_semaphore()

    @pl.loop(1, G)
    def _(r):
        pl.semaphore_signal(bar, inc=1, device_id=at_member(peer_of(me, r)), device_id_type=MESH)

    pl.semaphore_wait(bar, G - 1)

    def place(s):
        return out.at[:, pl.ds(s * SLAB, SLAB), pl.ds(pl.multiple_of(me * C, C), C)]

    def rows_for(s, p):
        return ob.at[s, pl.ds(pl.multiple_of(p * B, B), B)]

    def back(s, r):
        p = peer_of(me, r)
        return pltpu.make_async_remote_copy(
            src_ref=rows_for(s, p), dst_ref=place(s), send_sem=send_s.at[s, r], recv_sem=recv_s.at[s, r],
            device_id=at_member(p), device_id_type=MESH)

    def own(s):
        return pltpu.make_async_copy(rows_for(s, me), place(s), own_sem.at[s])

    for s in range(SLABS):
        load(s).wait()
        xf[...] = xin[s].astype(jnp.float32).reshape(N * SLAB, C)

        @pl.loop(0, SLAB // 2)
        def _(h):
            parts, means = [], []
            for q in range(2):
                x = xf[pl.ds(2 * h + q, N, stride=SLAB), :]
                mean = jnp.sum(x, axis=0, keepdims=True) * (1.0 / N)
                parts.append((x - mean).astype(jnp.bfloat16))
                means.append(mean)
            inc = jnp.dot(tt[...], jnp.concatenate(parts, axis=1), preferred_element_type=jnp.float32)
            for q in range(2):
                of[pl.ds(2 * h + q, N, stride=SLAB), :] = inc[:, q * C:(q + 1) * C] + means[q]

        ob[s] = of[...].reshape(N, SLAB, C).astype(jnp.bfloat16)
        for r in ORDER:
            back(s, r).start()
        own(s).start()

    for s in range(SLABS):
        own(s).wait()

        @pl.loop(1, G)
        def _(r):
            back(s, r).wait()


def apply_and_return(X, tt):
    vmem = pl.BlockSpec(memory_space=pltpu.VMEM)
    anym = pl.BlockSpec(memory_space=ANY)
    dma = pltpu.SemaphoreType.DMA
    return pl.pallas_call(
        apply_kernel,
        out_shape=jax.ShapeDtypeStruct((B, R, G * C), jnp.bfloat16),
        in_specs=[anym, vmem], out_specs=anym,
        scratch_shapes=[
            pltpu.VMEM((SLABS, N, SLAB, C), jnp.bfloat16),
            pltpu.VMEM((N * SLAB, C), jnp.float32),
            pltpu.VMEM((N * SLAB, C), jnp.float32),
            pltpu.VMEM((SLABS, N, SLAB, C), jnp.bfloat16),
            dma((SLABS,)), dma((SLABS,)), dma((SLABS, G)), dma((SLABS, G)),
        ],
        compiler_params=pltpu.CompilerParams(collective_id=1, has_side_effects=True, vmem_limit_bytes=48 << 20),
        name="apply_and_return",
    )(X, tt)


BULK_AT = (0, 3, 5, 8, 10, 31)


def local(prior, loc, tally, reading, sigma):
    usable = (lax.broadcasted_iota(jnp.int32, (1, OBS), 1) < tally[0, 0]).astype(jnp.float32)
    X, gram = gather_and_sum(prior, loc[0], reading[0], usable / sigma[0], BULK_AT)
    return apply_and_return(X, transform_rows(gram))


def solution(mesh):
    in_specs = (
        P("member", None, "grid"),
        P("grid", "member", None),
        P("grid", "member"),
        P("grid", "member", None),
        P("grid", "member", None),
    )
    return jax.shard_map(local, mesh=mesh, in_specs=in_specs, out_specs=P("member", None, "grid"), check_vma=False)
```

```python
import functools

import jax
import jax.numpy as jnp
from jax import lax
from jax.experimental import pallas as pl
from jax.experimental.pallas import tpu as pltpu
from jax.sharding import PartitionSpec as P

HIGHEST = lax.Precision.HIGHEST
MESH = pl.DeviceIdType.MESH
ANY = pl.ANY

N = 512
G = 32
B = N // G
Z = 8
R = 48
C = 128
OBS = 128
EXT = N + 128
SLAB = 8
SLABS = R // SLAB
CHIPS = G // 2
HALF = N // 2

ORDER = (8, 24, 16, 2, 6, 4, 1, 9, 25, 17, 3, 7, 5, 10, 26, 18, 11, 27, 19, 12, 28, 20, 13, 29, 21, 14, 30, 22, 15, 31, 23)


def peer_of(me, r):
    dx, dy, dc = r // 8, (r // 2) % 4, r % 2
    x, y, c = me // 8, (me // 2) % 4, me % 2
    s = 1 - 2 * c
    return ((x + s * dx + 4) % 4) * 8 + ((y + s * dy + 4) % 4) * 2 + (c + dc) % 2


def at_member(p):
    return {"member": p}


def at_grid(q):
    return {"grid": q}


def gather_kernel(bulk_at, prior, loc, val, scale, X, gram_out, tt, left, pv, locs, hxs, hxr, gl, half, rs, part, zr,
                  total, gram, m, local_sem, own_sem, bulk_s, bulk_r, loc_s, loc_r, hx_s, hx_r, pair_s, pair_r,
                  rs_s, rs_r, z_s, z_r, ag_s, ag_r):
    me = lax.axis_index("member")
    g = lax.axis_index("grid")
    chip, core = me // 2, me % 2
    row = pl.multiple_of(me * B, B)
    mine = pl.multiple_of(core * HALF, HALF)
    other = pl.multiple_of((1 - core) * HALF, HALF)
    share = pl.multiple_of(core * HALF + chip * B, B)

    def bulk(s, r):
        p = peer_of(me, r)
        return pltpu.make_async_remote_copy(
            src_ref=prior.at[:, pl.ds(pl.multiple_of(s * SLAB, SLAB), SLAB), pl.ds(pl.multiple_of(p * C, C), C)],
            dst_ref=X.at[s, pl.ds(row, B)],
            send_sem=bulk_s.at[s, r], recv_sem=bulk_r.at[s, r], device_id=at_member(p), device_id_type=MESH)

    def send_bulk(stage):
        for i in range(bulk_at[stage], bulk_at[stage + 1]):
            bulk(i // (G - 1), ORDER[i % (G - 1)]).start()

    def plane(src, dst, s, t, r):
        p = peer_of(me, r)
        return pltpu.make_async_remote_copy(
            src_ref=src(p), dst_ref=dst, send_sem=s.at[r], recv_sem=t.at[r],
            device_id=at_member(p), device_id_type=MESH)

    load = pltpu.make_async_copy(prior, pv, local_sem.at[0])
    load.start()

    bar = pltpu.get_barrier_semaphore()

    @pl.loop(1, G)
    def _(r):
        pl.semaphore_signal(bar, inc=1, device_id=at_member(peer_of(me, r)), device_id_type=MESH)

    @pl.loop(1, Z)
    def _(d):
        pl.semaphore_signal(bar, inc=1, device_id=at_grid((g + d) % Z), device_id_type=MESH)

    pl.semaphore_wait(bar, G - 1 + Z - 1)

    def loc_copy(r):
        return plane(lambda p: loc, locs.at[me], loc_s, loc_r, r)

    @pl.loop(1, G)
    def _(r):
        loc_copy(r).start()

    locs[me] = loc[...]
    send_bulk(0)
    load.wait()

    def own(s):
        return pltpu.make_async_copy(
            pv.at[:, pl.ds(pl.multiple_of(s * SLAB, SLAB), SLAB), pl.ds(pl.multiple_of(me * C, C), C)],
            X.at[s, pl.ds(row, B)], own_sem.at[s])

    for s in range(SLABS):
        own(s).start()

    @pl.loop(1, G)
    def _(r):
        loc_copy(r).wait()

    send_bulk(1)

    def hx_copy(r):
        return plane(lambda p: hxs.at[p], hxr.at[pl.ds(row, B)], hx_s, hx_r, r)

    def observe(b):
        cell = locs[b]
        lane = cell % C
        level = cell // C
        pick = (lax.broadcasted_iota(jnp.int32, (C, OBS), 0) == lane).astype(jnp.bfloat16)
        keep = lax.broadcasted_iota(jnp.int32, (R, OBS), 0) == level
        block = pv[:, :, pl.ds(pl.multiple_of(b * C, C), C)].reshape(B * R, C)
        both = jnp.dot(block, pick, preferred_element_type=jnp.float32).reshape(B, R, OBS)
        return jnp.sum(jnp.where(keep[None], both, 0.0), axis=1).astype(jnp.bfloat16)

    @pl.loop(1, G + 1)
    def _(r):
        @pl.when(r < G)
        def _():
            p = peer_of(me, r)
            hxs[p] = observe(p)

        @pl.when(r > 1)
        def _():
            hx_copy(r - 1).start()

    hxr[pl.ds(row, B), :] = observe(me)
    send_bulk(2)

    @pl.loop(1, G)
    def _(r):
        hx_copy(r).wait()

    hx = hxr[...].astype(jnp.float32)
    mean = jnp.sum(hx, axis=0, keepdims=True) * (1.0 / N)
    white = (hx - mean) * scale[...]
    innovation = (val[...] - mean) * scale[...]
    first = lax.broadcasted_iota(jnp.int32, (128, OBS), 0) == 0
    side = jnp.where(first, innovation, 0.0)
    last = (((1,), (1,)), ((), ()))
    for i in range(4):
        rows = pl.ds(i * 128, 128)
        w_i = white[i * 128:(i + 1) * 128]
        gl[rows, :N] = lax.dot_general(w_i, white, last, precision=HIGHEST, preferred_element_type=jnp.float32)
        gl[rows, N:] = lax.dot_general(w_i, side, last, precision=HIGHEST, preferred_element_type=jnp.float32)

    def pair_copy(i, src, dst):
        return pltpu.make_async_remote_copy(
            src_ref=src, dst_ref=dst, send_sem=pair_s.at[i], recv_sem=pair_r.at[i],
            device_id=at_member(chip * 2 + 1 - core), device_id_type=MESH)

    swap = pair_copy(0, gl.at[pl.ds(other, HALF)], half)
    swap.start()
    send_bulk(3)
    swap.wait()
    gl[pl.ds(mine, HALF), :] += half[...]

    def rs_copy(r):
        return plane(lambda p: gl.at[pl.ds(pl.multiple_of(core * HALF + (p // 2) * B, B), B)], rs.at[chip], rs_s, rs_r, 2 * r)

    @pl.loop(1, CHIPS)
    def _(r):
        rs_copy(r).start()

    rs[chip] = gl[pl.ds(share, B), :]
    send_bulk(4)

    @pl.loop(1, CHIPS)
    def _(r):
        rs_copy(r).wait()

    part[...] = lax.fori_loop(1, CHIPS, lambda i, t: t + rs[i], rs[0])

    def z_copy(d):
        return pltpu.make_async_remote_copy(
            src_ref=part, dst_ref=zr.at[g], send_sem=z_s.at[d], recv_sem=z_r.at[d],
            device_id=at_grid((g + d) % Z), device_id_type=MESH)

    zr[g] = part[...]

    @pl.loop(1, Z)
    def _(d):
        z_copy(d).start()

    send_bulk(5)

    @pl.loop(1, Z)
    def _(d):
        z_copy(d).wait()

    total[...] = lax.fori_loop(1, Z, lambda i, t: t + zr[i], zr[0])

    def ag_copy(r):
        return plane(lambda p: total, gram.at[pl.ds(share, B)], ag_s, ag_r, 2 * r)

    gram[pl.ds(share, B), :] = total[...]

    @pl.loop(1, CHIPS)
    def _(r):
        ag_copy(r).start()

    send_bulk(6)

    @pl.loop(1, CHIPS)
    def _(r):
        ag_copy(r).wait()

    swap = pair_copy(1, gram.at[pl.ds(mine, HALF)], gram.at[pl.ds(mine, HALF)])
    swap.start()
    send_bulk(7)
    swap.wait()
    start_factor(gram, m)
    for _ in range(COARSE):
        update_factor(gram, m, lax.Precision.DEFAULT)
    keep_gram = pltpu.make_async_copy(gram, gram_out, local_sem.at[1])
    keep_gram.start()
    for _ in range(FINE):
        rest = update_factor(gram, m, HIGHEST)
    left[...] = jnp.broadcast_to(rest, (8, 128))
    tt[...] = finish_factor(gram, m)

    keep_gram.wait()
    for s in range(SLABS):
        own(s).wait()

        @pl.loop(1, G)
        def _(r):
            bulk(s, r).wait()


def gather_and_sum(prior, loc, val, scale, bulk_at):
    vmem = pl.BlockSpec(memory_space=pltpu.VMEM)
    anym = pl.BlockSpec(memory_space=ANY)
    dma = pltpu.SemaphoreType.DMA
    return pl.pallas_call(
        functools.partial(gather_kernel, bulk_at),
        out_shape=(
            jax.ShapeDtypeStruct((SLABS, N, SLAB, C), jnp.bfloat16),
            jax.ShapeDtypeStruct((N, EXT), jnp.float32),
            jax.ShapeDtypeStruct((N, N), jnp.bfloat16),
            jax.ShapeDtypeStruct((8, 128), jnp.float32),
        ),
        in_specs=[anym, vmem, vmem, vmem],
        out_specs=(anym, anym, vmem, vmem),
        scratch_shapes=[
            pltpu.VMEM((B, R, G * C), jnp.bfloat16),
            pltpu.VMEM((G, 1, OBS), jnp.int32),
            pltpu.VMEM((G, B, OBS), jnp.bfloat16),
            pltpu.VMEM((N, OBS), jnp.bfloat16),
            pltpu.VMEM((N, EXT), jnp.float32),
            pltpu.VMEM((HALF, EXT), jnp.float32),
            pltpu.VMEM((CHIPS, B, EXT), jnp.float32),
            pltpu.VMEM((B, EXT), jnp.float32),
            pltpu.VMEM((Z, B, EXT), jnp.float32),
            pltpu.VMEM((B, EXT), jnp.float32),
            pltpu.VMEM((N, EXT), jnp.float32),
            pltpu.VMEM((N, N), jnp.float32),
            dma((2,)), dma((SLABS,)), dma((SLABS, G)), dma((SLABS, G)), dma((G,)), dma((G,)), dma((G,)), dma((G,)),
            dma((2,)), dma((2,)), dma((G,)), dma((G,)), dma((Z,)), dma((Z,)), dma((G,)), dma((G,)),
        ],
        compiler_params=pltpu.CompilerParams(collective_id=0, has_side_effects=True, vmem_limit_bytes=56 << 20),
        name="gather_and_sum",
    )(prior, loc, val, scale)


def diagonal_mask():
    return lax.broadcasted_iota(jnp.int32, (N, N), 0) == lax.broadcasted_iota(jnp.int32, (N, N), 1)


def start_factor(gram, m):
    same = diagonal_mask()
    a = gram[:, :N] + jnp.where(same, N - 1.0, 0.0)
    gram[:, :N] = a
    m[...] = jnp.where(same, lax.rsqrt(jnp.sum(jnp.where(same, a, 0.0), axis=1, keepdims=True)), 0.0)


def update_factor(gram, m, precision):
    t = jnp.dot(m[...], gram[:, :N], precision=precision, preferred_element_type=jnp.float32)
    e = lax.dot_general(t, m[...], (((1,), (1,)), ((), ())), precision=precision, preferred_element_type=jnp.float32)
    rows = lax.broadcasted_iota(jnp.int32, (N, N), 0)
    cols = lax.broadcasted_iota(jnp.int32, (N, N), 1)
    low = jnp.where(cols < rows, e, jnp.where(cols == rows, 0.5 * (e - 1.0), 0.0))
    m[...] -= jnp.dot(low, m[...], preferred_element_type=jnp.float32)
    return 2.0 * jnp.sum(low * low)


def finish_factor(gram, m):
    inner = jnp.dot(m[...], gram[:, N:], precision=HIGHEST, preferred_element_type=jnp.float32)
    weight = lax.dot_general(inner, m[...], (((0,), (0,)), ((), ())), precision=HIGHEST,
                             preferred_element_type=jnp.float32)[0:1]
    return (weight + jnp.sqrt(jnp.float32(N - 1.0)) * m[...]).astype(jnp.bfloat16)


def eliminate(a, m):
    m[...] = jnp.where(diagonal_mask(), 1.0, 0.0)

    @pl.loop(0, N)
    def _(k):
        pivot_row = a[pl.ds(k, 1), :N]
        lanes = lax.broadcasted_iota(jnp.int32, (1, N), 1)
        pivot = jnp.sum(jnp.where(lanes == k, pivot_row, 0.0), axis=1, keepdims=True)
        inv = 1.0 / jnp.sqrt(pivot)
        u = pivot_row * inv
        v = m[pl.ds(k, 1), :] * inv
        m[pl.ds(k, 1), :] = v

        @pl.loop(0, N // 64)
        def _(i):
            rows = pl.ds(pl.multiple_of(i * 64, 64), 64)
            blk = a[rows, :N]
            cols = lax.broadcasted_iota(jnp.int32, (64, N), 1)
            ids = lax.broadcasted_iota(jnp.int32, (64, 1), 0) + i * 64
            col = jnp.sum(jnp.where(cols == k, blk, 0.0), axis=1, keepdims=True) * inv
            col = jnp.where(ids > k, col, 0.0)
            a[rows, :N] = blk - col * u
            m[rows, :] = m[rows, :] - col * v


COARSE = 5
FINE = 2
TIGHT = 1e-5


def settle_kernel(left, gram, tt_in, tt, a, m, result, sem):
    @pl.when(jnp.logical_not(jnp.max(left[...]) <= TIGHT))
    def _():
        fetch = pltpu.make_async_copy(gram, a, sem)
        fetch.start()
        fetch.wait()
        eliminate(a, m)
        result[...] = finish_factor(a, m)
        store = pltpu.make_async_copy(result, tt, sem)
        store.start()
        store.wait()


def settle(left, gram, tt):
    vmem = pl.BlockSpec(memory_space=pltpu.VMEM)
    anym = pl.BlockSpec(memory_space=ANY)
    return pl.pallas_call(
        settle_kernel,
        out_shape=jax.ShapeDtypeStruct((N, N), jnp.bfloat16),
        in_specs=[vmem, anym, anym], out_specs=anym,
        scratch_shapes=[pltpu.VMEM((N, EXT), jnp.float32), pltpu.VMEM((N, N), jnp.float32),
                        pltpu.VMEM((N, N), jnp.bfloat16), pltpu.SemaphoreType.DMA],
        input_output_aliases={2: 0},
        compiler_params=pltpu.CompilerParams(vmem_limit_bytes=24 << 20),
        name="settle",
    )(left, gram, tt)


def apply_kernel(X, tt, out, xin, xf, of, ob, load_sem, own_sem, send_s, recv_s):
    me = lax.axis_index("member")

    def load(s):
        return pltpu.make_async_copy(X.at[s], xin.at[s], load_sem.at[s])

    for s in range(SLABS):
        load(s).start()

    bar = pltpu.get_barrier_semaphore()

    @pl.loop(1, G)
    def _(r):
        pl.semaphore_signal(bar, inc=1, device_id=at_member(peer_of(me, r)), device_id_type=MESH)

    pl.semaphore_wait(bar, G - 1)

    def place(s):
        return out.at[:, pl.ds(s * SLAB, SLAB), pl.ds(pl.multiple_of(me * C, C), C)]

    def rows_for(s, p):
        return ob.at[s, pl.ds(pl.multiple_of(p * B, B), B)]

    def back(s, r):
        p = peer_of(me, r)
        return pltpu.make_async_remote_copy(
            src_ref=rows_for(s, p), dst_ref=place(s), send_sem=send_s.at[s, r], recv_sem=recv_s.at[s, r],
            device_id=at_member(p), device_id_type=MESH)

    def own(s):
        return pltpu.make_async_copy(rows_for(s, me), place(s), own_sem.at[s])

    for s in range(SLABS):
        load(s).wait()
        xf[...] = xin[s].astype(jnp.float32).reshape(N * SLAB, C)

        @pl.loop(0, SLAB // 2)
        def _(h):
            parts, means = [], []
            for q in range(2):
                x = xf[pl.ds(2 * h + q, N, stride=SLAB), :]
                mean = jnp.sum(x, axis=0, keepdims=True) * (1.0 / N)
                parts.append((x - mean).astype(jnp.bfloat16))
                means.append(mean)
            inc = jnp.dot(tt[...], jnp.concatenate(parts, axis=1), preferred_element_type=jnp.float32)
            for q in range(2):
                of[pl.ds(2 * h + q, N, stride=SLAB), :] = inc[:, q * C:(q + 1) * C] + means[q]

        ob[s] = of[...].reshape(N, SLAB, C).astype(jnp.bfloat16)
        for r in ORDER:
            back(s, r).start()
        own(s).start()

    for s in range(SLABS):
        own(s).wait()

        @pl.loop(1, G)
        def _(r):
            back(s, r).wait()


def apply_and_return(X, tt):
    vmem = pl.BlockSpec(memory_space=pltpu.VMEM)
    anym = pl.BlockSpec(memory_space=ANY)
    dma = pltpu.SemaphoreType.DMA
    return pl.pallas_call(
        apply_kernel,
        out_shape=jax.ShapeDtypeStruct((B, R, G * C), jnp.bfloat16),
        in_specs=[anym, vmem], out_specs=anym,
        scratch_shapes=[
            pltpu.VMEM((SLABS, N, SLAB, C), jnp.bfloat16),
            pltpu.VMEM((N * SLAB, C), jnp.float32),
            pltpu.VMEM((N * SLAB, C), jnp.float32),
            pltpu.VMEM((SLABS, N, SLAB, C), jnp.bfloat16),
            dma((SLABS,)), dma((SLABS,)), dma((SLABS, G)), dma((SLABS, G)),
        ],
        compiler_params=pltpu.CompilerParams(collective_id=1, has_side_effects=True, vmem_limit_bytes=48 << 20),
        name="apply_and_return",
    )(X, tt)


BULK_AT = (0, 8, 20, 36, 44, 50, 76, 82, 186)


def local(prior, loc, tally, reading, sigma):
    usable = (lax.broadcasted_iota(jnp.int32, (1, OBS), 1) < tally[0, 0]).astype(jnp.float32)
    X, gram, tt, left = gather_and_sum(prior, loc[0], reading[0], usable / sigma[0], BULK_AT)
    return apply_and_return(X, settle(left, gram, tt))


def solution(mesh):
    in_specs = (
        P("member", None, "grid"),
        P("grid", "member", None),
        P("grid", "member"),
        P("grid", "member", None),
        P("grid", "member", None),
    )
    return jax.shard_map(local, mesh=mesh, in_specs=in_specs, out_specs=P("member", None, "grid"), check_vma=False)
```

```python
import functools

import jax
import jax.numpy as jnp
from jax import lax
from jax.experimental import pallas as pl
from jax.experimental.pallas import tpu as pltpu
from jax.sharding import PartitionSpec as P

HIGHEST = lax.Precision.HIGHEST
MESH = pl.DeviceIdType.MESH
ANY = pl.ANY

N = 512
G = 32
B = N // G
Z = 8
R = 48
C = 128
OBS = 128
EXT = N + 128
SLAB = 8
SLABS = R // SLAB
CHIPS = G // 2
HALF = N // 2

ORDER = (8, 24, 16, 2, 6, 4, 1, 9, 25, 17, 3, 7, 5, 10, 26, 18, 11, 27, 19, 12, 28, 20, 13, 29, 21, 14, 30, 22, 15, 31, 23)


def peer_of(me, r):
    dx, dy, dc = r // 8, (r // 2) % 4, r % 2
    x, y, c = me // 8, (me // 2) % 4, me % 2
    s = 1 - 2 * c
    return ((x + s * dx + 4) % 4) * 8 + ((y + s * dy + 4) % 4) * 2 + (c + dc) % 2


def at_member(p):
    return {"member": p}


def at_grid(q):
    return {"grid": q}


def gather_kernel(bulk_at, prior, loc, val, scale, X, gram_out, tt, left, pv, locs, hxs, hxr, gl, half, rs, part, zr,
                  total, gram, m, local_sem, own_sem, bulk_s, bulk_r, loc_s, loc_r, hx_s, hx_r, pair_s, pair_r,
                  rs_s, rs_r, z_s, z_r, ag_s, ag_r):
    me = lax.axis_index("member")
    g = lax.axis_index("grid")
    chip, core = me // 2, me % 2
    row = pl.multiple_of(me * B, B)
    mine = pl.multiple_of(core * HALF, HALF)
    other = pl.multiple_of((1 - core) * HALF, HALF)
    share = pl.multiple_of(core * HALF + chip * B, B)

    def bulk(s, r):
        p = peer_of(me, r)
        return pltpu.make_async_remote_copy(
            src_ref=prior.at[:, pl.ds(pl.multiple_of(s * SLAB, SLAB), SLAB), pl.ds(pl.multiple_of(p * C, C), C)],
            dst_ref=X.at[s, pl.ds(row, B)],
            send_sem=bulk_s.at[s, r], recv_sem=bulk_r.at[s, r], device_id=at_member(p), device_id_type=MESH)

    def send_bulk(stage):
        for i in range(bulk_at[stage], bulk_at[stage + 1]):
            bulk(i // (G - 1), ORDER[i % (G - 1)]).start()

    def plane(src, dst, s, t, r):
        p = peer_of(me, r)
        return pltpu.make_async_remote_copy(
            src_ref=src(p), dst_ref=dst, send_sem=s.at[r], recv_sem=t.at[r],
            device_id=at_member(p), device_id_type=MESH)

    load = pltpu.make_async_copy(prior, pv, local_sem.at[0])
    load.start()

    bar = pltpu.get_barrier_semaphore()

    @pl.loop(1, G)
    def _(r):
        pl.semaphore_signal(bar, inc=1, device_id=at_member(peer_of(me, r)), device_id_type=MESH)

    @pl.loop(1, Z)
    def _(d):
        pl.semaphore_signal(bar, inc=1, device_id=at_grid((g + d) % Z), device_id_type=MESH)

    pl.semaphore_wait(bar, G - 1 + Z - 1)

    def loc_copy(r):
        return plane(lambda p: loc, locs.at[me], loc_s, loc_r, r)

    @pl.loop(1, G)
    def _(r):
        loc_copy(r).start()

    locs[me] = loc[...]
    send_bulk(0)
    load.wait()

    def own(s):
        return pltpu.make_async_copy(
            pv.at[:, pl.ds(pl.multiple_of(s * SLAB, SLAB), SLAB), pl.ds(pl.multiple_of(me * C, C), C)],
            X.at[s, pl.ds(row, B)], own_sem.at[s])

    for s in range(SLABS):
        own(s).start()

    @pl.loop(1, G)
    def _(r):
        loc_copy(r).wait()

    send_bulk(1)

    def hx_copy(r):
        return plane(lambda p: hxs.at[p], hxr.at[pl.ds(row, B)], hx_s, hx_r, r)

    def observe(b):
        cell = locs[b]
        lane = cell % C
        level = cell // C
        pick = (lax.broadcasted_iota(jnp.int32, (C, OBS), 0) == lane).astype(jnp.bfloat16)
        keep = lax.broadcasted_iota(jnp.int32, (R, OBS), 0) == level
        block = pv[:, :, pl.ds(pl.multiple_of(b * C, C), C)].reshape(B * R, C)
        both = jnp.dot(block, pick, preferred_element_type=jnp.float32).reshape(B, R, OBS)
        return jnp.sum(jnp.where(keep[None], both, 0.0), axis=1).astype(jnp.bfloat16)

    @pl.loop(1, G + 1)
    def _(r):
        @pl.when(r < G)
        def _():
            p = peer_of(me, r)
            hxs[p] = observe(p)

        @pl.when(r > 1)
        def _():
            hx_copy(r - 1).start()

    hxr[pl.ds(row, B), :] = observe(me)
    send_bulk(2)

    @pl.loop(1, G)
    def _(r):
        hx_copy(r).wait()

    hx = hxr[...].astype(jnp.float32)
    mean = jnp.sum(hx, axis=0, keepdims=True) * (1.0 / N)
    white = (hx - mean) * scale[...]
    innovation = (val[...] - mean) * scale[...]
    first = lax.broadcasted_iota(jnp.int32, (128, OBS), 0) == 0
    side = jnp.where(first, innovation, 0.0)
    last = (((1,), (1,)), ((), ()))
    for i in range(4):
        rows = pl.ds(i * 128, 128)
        w_i = white[i * 128:(i + 1) * 128]
        gl[rows, :N] = lax.dot_general(w_i, white, last, precision=HIGHEST, preferred_element_type=jnp.float32)
        gl[rows, N:] = lax.dot_general(w_i, side, last, precision=HIGHEST, preferred_element_type=jnp.float32)

    def pair_copy(i, src, dst):
        return pltpu.make_async_remote_copy(
            src_ref=src, dst_ref=dst, send_sem=pair_s.at[i], recv_sem=pair_r.at[i],
            device_id=at_member(chip * 2 + 1 - core), device_id_type=MESH)

    swap = pair_copy(0, gl.at[pl.ds(other, HALF)], half)
    swap.start()
    send_bulk(3)
    swap.wait()
    gl[pl.ds(mine, HALF), :] += half[...]

    def rs_copy(r):
        return plane(lambda p: gl.at[pl.ds(pl.multiple_of(core * HALF + (p // 2) * B, B), B)], rs.at[chip], rs_s, rs_r, 2 * r)

    @pl.loop(1, CHIPS)
    def _(r):
        rs_copy(r).start()

    rs[chip] = gl[pl.ds(share, B), :]
    send_bulk(4)

    @pl.loop(1, CHIPS)
    def _(r):
        rs_copy(r).wait()

    part[...] = lax.fori_loop(1, CHIPS, lambda i, t: t + rs[i], rs[0])

    def z_copy(d):
        return pltpu.make_async_remote_copy(
            src_ref=part, dst_ref=zr.at[g], send_sem=z_s.at[d], recv_sem=z_r.at[d],
            device_id=at_grid((g + d) % Z), device_id_type=MESH)

    zr[g] = part[...]

    @pl.loop(1, Z)
    def _(d):
        z_copy(d).start()

    send_bulk(5)

    @pl.loop(1, Z)
    def _(d):
        z_copy(d).wait()

    total[...] = lax.fori_loop(1, Z, lambda i, t: t + zr[i], zr[0])

    def ag_copy(r):
        return plane(lambda p: total, gram.at[pl.ds(share, B)], ag_s, ag_r, 2 * r)

    gram[pl.ds(share, B), :] = total[...]

    @pl.loop(1, CHIPS)
    def _(r):
        ag_copy(r).start()

    send_bulk(6)

    @pl.loop(1, CHIPS)
    def _(r):
        ag_copy(r).wait()

    swap = pair_copy(1, gram.at[pl.ds(mine, HALF)], gram.at[pl.ds(mine, HALF)])
    swap.start()
    send_bulk(7)
    swap.wait()
    start_factor(gram, m)
    for _ in range(COARSE):
        update_factor(gram, m, lax.Precision.DEFAULT)
    keep_gram = pltpu.make_async_copy(gram, gram_out, local_sem.at[1])
    keep_gram.start()
    for _ in range(FINE):
        rest = update_factor(gram, m, HIGHEST)
    left[...] = jnp.broadcast_to(rest, (8, 128))
    tt[...] = finish_factor(gram, m)

    keep_gram.wait()
    for s in range(SLABS):
        own(s).wait()

        @pl.loop(1, G)
        def _(r):
            bulk(s, r).wait()


def gather_and_sum(prior, loc, val, scale, bulk_at):
    vmem = pl.BlockSpec(memory_space=pltpu.VMEM)
    anym = pl.BlockSpec(memory_space=ANY)
    dma = pltpu.SemaphoreType.DMA
    return pl.pallas_call(
        functools.partial(gather_kernel, bulk_at),
        out_shape=(
            jax.ShapeDtypeStruct((SLABS, N, SLAB, C), jnp.bfloat16),
            jax.ShapeDtypeStruct((N, EXT), jnp.float32),
            jax.ShapeDtypeStruct((N, N), jnp.bfloat16),
            jax.ShapeDtypeStruct((8, 128), jnp.float32),
        ),
        in_specs=[anym, vmem, vmem, vmem],
        out_specs=(anym, anym, vmem, vmem),
        scratch_shapes=[
            pltpu.VMEM((B, R, G * C), jnp.bfloat16),
            pltpu.VMEM((G, 1, OBS), jnp.int32),
            pltpu.VMEM((G, B, OBS), jnp.bfloat16),
            pltpu.VMEM((N, OBS), jnp.bfloat16),
            pltpu.VMEM((N, EXT), jnp.float32),
            pltpu.VMEM((HALF, EXT), jnp.float32),
            pltpu.VMEM((CHIPS, B, EXT), jnp.float32),
            pltpu.VMEM((B, EXT), jnp.float32),
            pltpu.VMEM((Z, B, EXT), jnp.float32),
            pltpu.VMEM((B, EXT), jnp.float32),
            pltpu.VMEM((N, EXT), jnp.float32),
            pltpu.VMEM((N, N), jnp.float32),
            dma((2,)), dma((SLABS,)), dma((SLABS, G)), dma((SLABS, G)), dma((G,)), dma((G,)), dma((G,)), dma((G,)),
            dma((2,)), dma((2,)), dma((G,)), dma((G,)), dma((Z,)), dma((Z,)), dma((G,)), dma((G,)),
        ],
        compiler_params=pltpu.CompilerParams(collective_id=0, has_side_effects=True, vmem_limit_bytes=56 << 20),
        name="gather_and_sum",
    )(prior, loc, val, scale)


def diagonal_mask():
    return lax.broadcasted_iota(jnp.int32, (N, N), 0) == lax.broadcasted_iota(jnp.int32, (N, N), 1)


def start_factor(gram, m):
    same = diagonal_mask()
    a = gram[:, :N] + jnp.where(same, N - 1.0, 0.0)
    gram[:, :N] = a
    m[...] = jnp.where(same, lax.rsqrt(jnp.sum(jnp.where(same, a, 0.0), axis=1, keepdims=True)), 0.0)


def update_factor(gram, m, precision):
    t = jnp.dot(m[...], gram[:, :N], precision=precision, preferred_element_type=jnp.float32)
    e = lax.dot_general(t, m[...], (((1,), (1,)), ((), ())), precision=precision, preferred_element_type=jnp.float32)
    rows = lax.broadcasted_iota(jnp.int32, (N, N), 0)
    cols = lax.broadcasted_iota(jnp.int32, (N, N), 1)
    low = jnp.where(cols < rows, e, jnp.where(cols == rows, 0.5 * (e - 1.0), 0.0))
    m[...] -= jnp.dot(low, m[...], preferred_element_type=jnp.float32)
    return 2.0 * jnp.sum(low * low)


def finish_factor(gram, m):
    inner = jnp.dot(m[...], gram[:, N:], precision=HIGHEST, preferred_element_type=jnp.float32)
    weight = lax.dot_general(inner, m[...], (((0,), (0,)), ((), ())), precision=HIGHEST,
                             preferred_element_type=jnp.float32)[0:1]
    return (weight + jnp.sqrt(jnp.float32(N - 1.0)) * m[...]).astype(jnp.bfloat16)


def eliminate(a, m):
    m[...] = jnp.where(diagonal_mask(), 1.0, 0.0)

    @pl.loop(0, N)
    def _(k):
        pivot_row = a[pl.ds(k, 1), :N]
        lanes = lax.broadcasted_iota(jnp.int32, (1, N), 1)
        pivot = jnp.sum(jnp.where(lanes == k, pivot_row, 0.0), axis=1, keepdims=True)
        inv = 1.0 / jnp.sqrt(pivot)
        u = pivot_row * inv
        v = m[pl.ds(k, 1), :] * inv
        m[pl.ds(k, 1), :] = v

        @pl.loop(0, N // 64)
        def _(i):
            rows = pl.ds(pl.multiple_of(i * 64, 64), 64)
            blk = a[rows, :N]
            cols = lax.broadcasted_iota(jnp.int32, (64, N), 1)
            ids = lax.broadcasted_iota(jnp.int32, (64, 1), 0) + i * 64
            col = jnp.sum(jnp.where(cols == k, blk, 0.0), axis=1, keepdims=True) * inv
            col = jnp.where(ids > k, col, 0.0)
            a[rows, :N] = blk - col * u
            m[rows, :] = m[rows, :] - col * v


COARSE = 5
FINE = 2
TIGHT = 1e-5


def settle_kernel(left, gram, tt_in, tt, rest, a, m, result, sem):
    look = pltpu.make_async_copy(left, rest, sem)
    look.start()
    look.wait()

    @pl.when(jnp.logical_not(jnp.max(rest[...]) <= TIGHT))
    def _():
        fetch = pltpu.make_async_copy(gram, a, sem)
        fetch.start()
        fetch.wait()
        eliminate(a, m)
        result[...] = finish_factor(a, m)
        store = pltpu.make_async_copy(result, tt, sem)
        store.start()
        store.wait()


def settle(left, gram, tt):
    anym = pl.BlockSpec(memory_space=pltpu.HBM)
    return pl.pallas_call(
        settle_kernel,
        out_shape=jax.ShapeDtypeStruct((N, N), jnp.bfloat16),
        in_specs=[anym, anym, anym], out_specs=anym,
        scratch_shapes=[pltpu.VMEM((8, 128), jnp.float32), pltpu.VMEM((N, EXT), jnp.float32), pltpu.VMEM((N, N), jnp.float32),
                        pltpu.VMEM((N, N), jnp.bfloat16), pltpu.SemaphoreType.DMA],
        input_output_aliases={2: 0},
        compiler_params=pltpu.CompilerParams(vmem_limit_bytes=66_900_000),
        name="settle",
    )(left, gram, tt)


def apply_kernel(X, tt_hbm, out, tt, xin, xf, of, ob, tt_sem, load_sem, own_sem, send_s, recv_s):
    me = lax.axis_index("member")

    def load(s):
        return pltpu.make_async_copy(X.at[s], xin.at[s], load_sem.at[s])

    load(0).start()
    fetch = pltpu.make_async_copy(tt_hbm, tt, tt_sem)
    fetch.start()
    for s in range(1, SLABS):
        load(s).start()

    bar = pltpu.get_barrier_semaphore()

    @pl.loop(1, G)
    def _(r):
        pl.semaphore_signal(bar, inc=1, device_id=at_member(peer_of(me, r)), device_id_type=MESH)

    pl.semaphore_wait(bar, G - 1)

    def place(s):
        return out.at[:, pl.ds(s * SLAB, SLAB), pl.ds(pl.multiple_of(me * C, C), C)]

    def rows_for(s, p):
        return ob.at[s, pl.ds(pl.multiple_of(p * B, B), B)]

    def back(s, r):
        p = peer_of(me, r)
        return pltpu.make_async_remote_copy(
            src_ref=rows_for(s, p), dst_ref=place(s), send_sem=send_s.at[s, r], recv_sem=recv_s.at[s, r],
            device_id=at_member(p), device_id_type=MESH)

    def own(s):
        return pltpu.make_async_copy(rows_for(s, me), place(s), own_sem.at[s])

    fetch.wait()
    for s in range(SLABS):
        load(s).wait()
        xf[...] = xin[s].astype(jnp.float32).reshape(N * SLAB, C)

        @pl.loop(0, SLAB // 2)
        def _(h):
            parts, means = [], []
            for q in range(2):
                x = xf[pl.ds(2 * h + q, N, stride=SLAB), :]
                mean = jnp.sum(x, axis=0, keepdims=True) * (1.0 / N)
                parts.append((x - mean).astype(jnp.bfloat16))
                means.append(mean)
            inc = jnp.dot(tt[...], jnp.concatenate(parts, axis=1), preferred_element_type=jnp.float32)
            for q in range(2):
                of[pl.ds(2 * h + q, N, stride=SLAB), :] = inc[:, q * C:(q + 1) * C] + means[q]

        ob[s] = of[...].reshape(N, SLAB, C).astype(jnp.bfloat16)
        for r in ORDER:
            back(s, r).start()
        own(s).start()

    for s in range(SLABS):
        own(s).wait()

        @pl.loop(1, G)
        def _(r):
            back(s, r).wait()


def apply_and_return(X, tt):
    hbm = pl.BlockSpec(memory_space=pltpu.HBM)
    dma = pltpu.SemaphoreType.DMA
    return pl.pallas_call(
        apply_kernel,
        out_shape=pltpu.VMEM((B, R, G * C), jnp.bfloat16),
        in_specs=[hbm, hbm], out_specs=pl.BlockSpec(memory_space=pltpu.VMEM),
        scratch_shapes=[
            pltpu.VMEM((N, N), jnp.bfloat16),
            pltpu.VMEM((SLABS, N, SLAB, C), jnp.bfloat16),
            pltpu.VMEM((N * SLAB, C), jnp.float32),
            pltpu.VMEM((N * SLAB, C), jnp.float32),
            pltpu.VMEM((SLABS, N, SLAB, C), jnp.bfloat16),
            dma, dma((SLABS,)), dma((SLABS,)), dma((SLABS, G)), dma((SLABS, G)),
        ],
        compiler_params=pltpu.CompilerParams(collective_id=1, has_side_effects=True, vmem_limit_bytes=60_600_000),
        name="apply_and_return",
    )(X, tt)


BULK_AT = (0, 16, 40, 60, 84, 100, 130, 146, 186)


def local(prior, loc, tally, reading, sigma):
    usable = (lax.broadcasted_iota(jnp.int32, (1, OBS), 1) < tally[0, 0]).astype(jnp.float32)
    X, gram, tt, left = gather_and_sum(prior, loc[0], reading[0], usable / sigma[0], BULK_AT)
    return apply_and_return(X, settle(left, gram, tt))


def solution(mesh):
    in_specs = (
        P("member", None, "grid"),
        P("grid", "member", None),
        P("grid", "member"),
        P("grid", "member", None),
        P("grid", "member", None),
    )
    return jax.shard_map(local, mesh=mesh, in_specs=in_specs, out_specs=P("member", None, "grid"), check_vma=False)
```

```python
import functools

import jax
import jax.numpy as jnp
from jax import lax
from jax.experimental import pallas as pl
from jax.experimental.pallas import tpu as pltpu
from jax.sharding import PartitionSpec as P

HIGHEST = lax.Precision.HIGHEST
MESH = pl.DeviceIdType.MESH
ANY = pl.ANY

N = 512
G = 32
B = N // G
Z = 8
R = 48
C = 128
OBS = 128
EXT = N + 128
SLAB = 8
SLABS = R // SLAB
CHIPS = G // 2
HALF = N // 2

ORDER = (8, 24, 16, 2, 6, 4, 1, 9, 25, 17, 3, 7, 5, 10, 26, 18, 11, 27, 19, 12, 28, 20, 13, 29, 21, 14, 30, 22, 15, 31, 23)


def peer_of(me, r):
    dx, dy, dc = r // 8, (r // 2) % 4, r % 2
    x, y, c = me // 8, (me // 2) % 4, me % 2
    s = 1 - 2 * c
    return ((x + s * dx + 4) % 4) * 8 + ((y + s * dy + 4) % 4) * 2 + (c + dc) % 2


def at_member(p):
    return {"member": p}


def at_grid(q):
    return {"grid": q}


def gather_kernel(bulk_at, prior, loc, val, scale, X, gram_out, tt, left, pv, locs, hxs, hxr, gl, half, rs, part, zr,
                  total, gram, m, local_sem, own_sem, bulk_s, bulk_r, loc_s, loc_r, hx_s, hx_r, pair_s, pair_r,
                  rs_s, rs_r, z_s, z_r, ag_s, ag_r):
    me = lax.axis_index("member")
    g = lax.axis_index("grid")
    chip, core = me // 2, me % 2
    row = pl.multiple_of(me * B, B)
    mine = pl.multiple_of(core * HALF, HALF)
    other = pl.multiple_of((1 - core) * HALF, HALF)
    share = pl.multiple_of(core * HALF + chip * B, B)

    def bulk(s, r):
        p = peer_of(me, r)
        return pltpu.make_async_remote_copy(
            src_ref=prior.at[:, pl.ds(pl.multiple_of(s * SLAB, SLAB), SLAB), pl.ds(pl.multiple_of(p * C, C), C)],
            dst_ref=X.at[s, pl.ds(row, B)],
            send_sem=bulk_s.at[s, r], recv_sem=bulk_r.at[s, r], device_id=at_member(p), device_id_type=MESH)

    def send_bulk(stage):
        for i in range(bulk_at[stage], bulk_at[stage + 1]):
            bulk(i // (G - 1), ORDER[i % (G - 1)]).start()

    def plane(src, dst, s, t, r):
        p = peer_of(me, r)
        return pltpu.make_async_remote_copy(
            src_ref=src(p), dst_ref=dst, send_sem=s.at[r], recv_sem=t.at[r],
            device_id=at_member(p), device_id_type=MESH)

    load = pltpu.make_async_copy(prior, pv, local_sem.at[0])
    load.start()

    bar = pltpu.get_barrier_semaphore()

    @pl.loop(1, G)
    def _(r):
        pl.semaphore_signal(bar, inc=1, device_id=at_member(peer_of(me, r)), device_id_type=MESH)

    @pl.loop(1, Z)
    def _(d):
        pl.semaphore_signal(bar, inc=1, device_id=at_grid((g + d) % Z), device_id_type=MESH)

    pl.semaphore_wait(bar, G - 1 + Z - 1)

    def loc_copy(r):
        return plane(lambda p: loc, locs.at[me], loc_s, loc_r, r)

    @pl.loop(1, G)
    def _(r):
        loc_copy(r).start()

    locs[me] = loc[...]
    send_bulk(0)
    load.wait()

    def own(s):
        return pltpu.make_async_copy(
            pv.at[:, pl.ds(pl.multiple_of(s * SLAB, SLAB), SLAB), pl.ds(pl.multiple_of(me * C, C), C)],
            X.at[s, pl.ds(row, B)], own_sem.at[s])

    for s in range(SLABS):
        own(s).start()

    @pl.loop(1, G)
    def _(r):
        loc_copy(r).wait()

    send_bulk(1)

    def hx_copy(r):
        return plane(lambda p: hxs.at[p], hxr.at[pl.ds(row, B)], hx_s, hx_r, r)

    def observe(b):
        cell = locs[b]
        lane = cell % C
        level = cell // C
        pick = (lax.broadcasted_iota(jnp.int32, (C, OBS), 0) == lane).astype(jnp.bfloat16)
        keep = lax.broadcasted_iota(jnp.int32, (R, OBS), 0) == level
        block = pv[:, :, pl.ds(pl.multiple_of(b * C, C), C)].reshape(B * R, C)
        both = jnp.dot(block, pick, preferred_element_type=jnp.float32).reshape(B, R, OBS)
        return jnp.sum(jnp.where(keep[None], both, 0.0), axis=1).astype(jnp.bfloat16)

    @pl.loop(1, G + 1)
    def _(r):
        @pl.when(r < G)
        def _():
            p = peer_of(me, r)
            hxs[p] = observe(p)

        @pl.when(r > 1)
        def _():
            hx_copy(r - 1).start()

    hxr[pl.ds(row, B), :] = observe(me)
    send_bulk(2)

    @pl.loop(1, G)
    def _(r):
        hx_copy(r).wait()

    hx = hxr[...].astype(jnp.float32)
    mean = jnp.sum(hx, axis=0, keepdims=True) * (1.0 / N)
    white = (hx - mean) * scale[...]
    innovation = (val[...] - mean) * scale[...]
    first = lax.broadcasted_iota(jnp.int32, (128, OBS), 0) == 0
    side = jnp.where(first, innovation, 0.0)
    last = (((1,), (1,)), ((), ()))
    for i in range(4):
        rows = pl.ds(i * 128, 128)
        w_i = white[i * 128:(i + 1) * 128]
        gl[rows, :N] = lax.dot_general(w_i, white, last, precision=HIGHEST, preferred_element_type=jnp.float32)
        gl[rows, N:] = lax.dot_general(w_i, side, last, precision=HIGHEST, preferred_element_type=jnp.float32)

    def pair_copy(i, src, dst):
        return pltpu.make_async_remote_copy(
            src_ref=src, dst_ref=dst, send_sem=pair_s.at[i], recv_sem=pair_r.at[i],
            device_id=at_member(chip * 2 + 1 - core), device_id_type=MESH)

    swap = pair_copy(0, gl.at[pl.ds(other, HALF)], half)
    swap.start()
    send_bulk(3)
    swap.wait()
    gl[pl.ds(mine, HALF), :] += half[...]

    def rs_copy(r):
        return plane(lambda p: gl.at[pl.ds(pl.multiple_of(core * HALF + (p // 2) * B, B), B)], rs.at[chip], rs_s, rs_r, 2 * r)

    @pl.loop(1, CHIPS)
    def _(r):
        rs_copy(r).start()

    rs[chip] = gl[pl.ds(share, B), :]
    send_bulk(4)

    @pl.loop(1, CHIPS)
    def _(r):
        rs_copy(r).wait()

    part[...] = lax.fori_loop(1, CHIPS, lambda i, t: t + rs[i], rs[0])

    def z_copy(d):
        return pltpu.make_async_remote_copy(
            src_ref=part, dst_ref=zr.at[g], send_sem=z_s.at[d], recv_sem=z_r.at[d],
            device_id=at_grid((g + d) % Z), device_id_type=MESH)

    zr[g] = part[...]

    @pl.loop(1, Z)
    def _(d):
        z_copy(d).start()

    send_bulk(5)

    @pl.loop(1, Z)
    def _(d):
        z_copy(d).wait()

    total[...] = lax.fori_loop(1, Z, lambda i, t: t + zr[i], zr[0])

    def ag_copy(r):
        return plane(lambda p: total, gram.at[pl.ds(share, B)], ag_s, ag_r, 2 * r)

    gram[pl.ds(share, B), :] = total[...]

    @pl.loop(1, CHIPS)
    def _(r):
        ag_copy(r).start()

    send_bulk(6)

    @pl.loop(1, CHIPS)
    def _(r):
        ag_copy(r).wait()

    swap = pair_copy(1, gram.at[pl.ds(mine, HALF)], gram.at[pl.ds(mine, HALF)])
    swap.start()
    send_bulk(7)
    swap.wait()
    start_factor(gram, m)
    for _ in range(COARSE):
        update_factor(gram, m, lax.Precision.DEFAULT)
    keep_gram = pltpu.make_async_copy(gram, gram_out, local_sem.at[1])
    keep_gram.start()
    for _ in range(FINE):
        rest = update_factor(gram, m, HIGHEST)
    left[...] = jnp.broadcast_to(rest, (8, 128))
    tt[...] = finish_factor(gram, m)

    keep_gram.wait()
    for s in range(SLABS):
        own(s).wait()

        @pl.loop(1, G)
        def _(r):
            bulk(s, r).wait()


def gather_and_sum(prior, loc, val, scale, bulk_at):
    vmem = pl.BlockSpec(memory_space=pltpu.VMEM)
    anym = pl.BlockSpec(memory_space=ANY)
    dma = pltpu.SemaphoreType.DMA
    return pl.pallas_call(
        functools.partial(gather_kernel, bulk_at),
        out_shape=(
            jax.ShapeDtypeStruct((SLABS, N, SLAB, C), jnp.bfloat16),
            jax.ShapeDtypeStruct((N, EXT), jnp.float32),
            jax.ShapeDtypeStruct((N, N), jnp.bfloat16),
            jax.ShapeDtypeStruct((8, 128), jnp.float32),
        ),
        in_specs=[anym, vmem, vmem, vmem],
        out_specs=(anym, anym, vmem, vmem),
        scratch_shapes=[
            pltpu.VMEM((B, R, G * C), jnp.bfloat16),
            pltpu.VMEM((G, 1, OBS), jnp.int32),
            pltpu.VMEM((G, B, OBS), jnp.bfloat16),
            pltpu.VMEM((N, OBS), jnp.bfloat16),
            pltpu.VMEM((N, EXT), jnp.float32),
            pltpu.VMEM((HALF, EXT), jnp.float32),
            pltpu.VMEM((CHIPS, B, EXT), jnp.float32),
            pltpu.VMEM((B, EXT), jnp.float32),
            pltpu.VMEM((Z, B, EXT), jnp.float32),
            pltpu.VMEM((B, EXT), jnp.float32),
            pltpu.VMEM((N, EXT), jnp.float32),
            pltpu.VMEM((N, N), jnp.float32),
            dma((2,)), dma((SLABS,)), dma((SLABS, G)), dma((SLABS, G)), dma((G,)), dma((G,)), dma((G,)), dma((G,)),
            dma((2,)), dma((2,)), dma((G,)), dma((G,)), dma((Z,)), dma((Z,)), dma((G,)), dma((G,)),
        ],
        compiler_params=pltpu.CompilerParams(collective_id=0, has_side_effects=True, vmem_limit_bytes=56 << 20),
        name="gather_and_sum",
    )(prior, loc, val, scale)


def diagonal_mask():
    return lax.broadcasted_iota(jnp.int32, (N, N), 0) == lax.broadcasted_iota(jnp.int32, (N, N), 1)


def start_factor(gram, m):
    same = diagonal_mask()
    a = gram[:, :N] + jnp.where(same, N - 1.0, 0.0)
    gram[:, :N] = a
    m[...] = jnp.where(same, lax.rsqrt(jnp.sum(jnp.where(same, a, 0.0), axis=1, keepdims=True)), 0.0)


def update_factor(gram, m, precision):
    t = jnp.dot(m[...], gram[:, :N], precision=precision, preferred_element_type=jnp.float32)
    e = lax.dot_general(t, m[...], (((1,), (1,)), ((), ())), precision=precision, preferred_element_type=jnp.float32)
    rows = lax.broadcasted_iota(jnp.int32, (N, N), 0)
    cols = lax.broadcasted_iota(jnp.int32, (N, N), 1)
    low = jnp.where(cols < rows, e, jnp.where(cols == rows, 0.5 * (e - 1.0), 0.0))
    m[...] -= jnp.dot(low, m[...], preferred_element_type=jnp.float32)
    return 2.0 * jnp.sum(low * low)


def finish_factor(gram, m):
    inner = jnp.dot(m[...], gram[:, N:], precision=HIGHEST, preferred_element_type=jnp.float32)
    weight = lax.dot_general(inner, m[...], (((0,), (0,)), ((), ())), precision=HIGHEST,
                             preferred_element_type=jnp.float32)[0:1]
    return (weight + jnp.sqrt(jnp.float32(N - 1.0)) * m[...]).astype(jnp.bfloat16)


def eliminate(a, m):
    m[...] = jnp.where(diagonal_mask(), 1.0, 0.0)

    @pl.loop(0, N)
    def _(k):
        pivot_row = a[pl.ds(k, 1), :N]
        lanes = lax.broadcasted_iota(jnp.int32, (1, N), 1)
        pivot = jnp.sum(jnp.where(lanes == k, pivot_row, 0.0), axis=1, keepdims=True)
        inv = 1.0 / jnp.sqrt(pivot)
        u = pivot_row * inv
        v = m[pl.ds(k, 1), :] * inv
        m[pl.ds(k, 1), :] = v

        @pl.loop(0, N // 64)
        def _(i):
            rows = pl.ds(pl.multiple_of(i * 64, 64), 64)
            blk = a[rows, :N]
            cols = lax.broadcasted_iota(jnp.int32, (64, N), 1)
            ids = lax.broadcasted_iota(jnp.int32, (64, 1), 0) + i * 64
            col = jnp.sum(jnp.where(cols == k, blk, 0.0), axis=1, keepdims=True) * inv
            col = jnp.where(ids > k, col, 0.0)
            a[rows, :N] = blk - col * u
            m[rows, :] = m[rows, :] - col * v


COARSE = 5
FINE = 2
TIGHT = 1e-5


def settle_kernel(left, gram, tt_in, tt, rest, a, m, result, sem):
    look = pltpu.make_async_copy(left, rest, sem)
    look.start()
    look.wait()

    @pl.when(jnp.logical_not(jnp.max(rest[...]) <= TIGHT))
    def _():
        fetch = pltpu.make_async_copy(gram, a, sem)
        fetch.start()
        fetch.wait()
        eliminate(a, m)
        result[...] = finish_factor(a, m)
        store = pltpu.make_async_copy(result, tt, sem)
        store.start()
        store.wait()


def settle(left, gram, tt):
    anym = pl.BlockSpec(memory_space=pltpu.HBM)
    return pl.pallas_call(
        settle_kernel,
        out_shape=jax.ShapeDtypeStruct((N, N), jnp.bfloat16),
        in_specs=[anym, anym, anym], out_specs=anym,
        scratch_shapes=[pltpu.VMEM((8, 128), jnp.float32), pltpu.VMEM((N, EXT), jnp.float32), pltpu.VMEM((N, N), jnp.float32),
                        pltpu.VMEM((N, N), jnp.bfloat16), pltpu.SemaphoreType.DMA],
        input_output_aliases={2: 0},
        compiler_params=pltpu.CompilerParams(vmem_limit_bytes=66_900_000),
        name="settle",
    )(left, gram, tt)


def apply_kernel(X, tt_hbm, out, tt, xin, xf, of, ob, tt_sem, load_sem, own_sem, send_s, recv_s):
    me = lax.axis_index("member")

    def load(s):
        return pltpu.make_async_copy(X.at[s], xin.at[s], load_sem.at[s])

    load(0).start()
    fetch = pltpu.make_async_copy(tt_hbm, tt, tt_sem)
    fetch.start()
    for s in range(1, SLABS):
        load(s).start()

    bar = pltpu.get_barrier_semaphore()

    @pl.loop(1, G)
    def _(r):
        pl.semaphore_signal(bar, inc=1, device_id=at_member(peer_of(me, r)), device_id_type=MESH)

    pl.semaphore_wait(bar, G - 1)

    def place(s):
        return out.at[:, pl.ds(s * SLAB, SLAB), pl.ds(pl.multiple_of(me * C, C), C)]

    def rows_for(s, p):
        return ob.at[s, pl.ds(pl.multiple_of(p * B, B), B)]

    def back(s, r):
        p = peer_of(me, r)
        return pltpu.make_async_remote_copy(
            src_ref=rows_for(s, p), dst_ref=place(s), send_sem=send_s.at[s, r], recv_sem=recv_s.at[s, r],
            device_id=at_member(p), device_id_type=MESH)

    def own(s):
        return pltpu.make_async_copy(rows_for(s, me), place(s), own_sem.at[s])

    fetch.wait()
    for s in range(SLABS):
        load(s).wait()
        xf[...] = xin[s].astype(jnp.float32).reshape(N * SLAB, C)

        @pl.loop(0, SLAB // 2)
        def _(h):
            parts, means = [], []
            for q in range(2):
                x = xf[pl.ds(2 * h + q, N, stride=SLAB), :]
                mean = jnp.sum(x, axis=0, keepdims=True) * (1.0 / N)
                parts.append((x - mean).astype(jnp.bfloat16))
                means.append(mean)
            inc = jnp.dot(tt[...], jnp.concatenate(parts, axis=1), preferred_element_type=jnp.float32)
            for q in range(2):
                of[pl.ds(2 * h + q, N, stride=SLAB), :] = inc[:, q * C:(q + 1) * C] + means[q]

        ob[s] = of[...].reshape(N, SLAB, C).astype(jnp.bfloat16)
        for r in ORDER:
            back(s, r).start()
        own(s).start()

    for s in range(SLABS):
        own(s).wait()

        @pl.loop(1, G)
        def _(r):
            back(s, r).wait()


def apply_and_return(X, tt):
    hbm = pl.BlockSpec(memory_space=pltpu.HBM)
    dma = pltpu.SemaphoreType.DMA
    return pl.pallas_call(
        apply_kernel,
        out_shape=pltpu.VMEM((B, R, G * C), jnp.bfloat16),
        in_specs=[hbm, hbm], out_specs=pl.BlockSpec(memory_space=pltpu.VMEM),
        scratch_shapes=[
            pltpu.VMEM((N, N), jnp.bfloat16),
            pltpu.VMEM((SLABS, N, SLAB, C), jnp.bfloat16),
            pltpu.VMEM((N * SLAB, C), jnp.float32),
            pltpu.VMEM((N * SLAB, C), jnp.float32),
            pltpu.VMEM((SLABS, N, SLAB, C), jnp.bfloat16),
            dma, dma((SLABS,)), dma((SLABS,)), dma((SLABS, G)), dma((SLABS, G)),
        ],
        compiler_params=pltpu.CompilerParams(collective_id=1, has_side_effects=True, vmem_limit_bytes=60_600_000),
        name="apply_and_return",
    )(X, tt)


BULK_AT = (0, 14, 38, 56, 74, 84, 120, 130, 186)


def local(prior, loc, tally, reading, sigma):
    usable = (lax.broadcasted_iota(jnp.int32, (1, OBS), 1) < tally[0, 0]).astype(jnp.float32)
    X, gram, tt, left = gather_and_sum(prior, loc[0], reading[0], usable / sigma[0], BULK_AT)
    return apply_and_return(X, settle(left, gram, tt))


def solution(mesh):
    in_specs = (
        P("member", None, "grid"),
        P("grid", "member", None),
        P("grid", "member"),
        P("grid", "member", None),
        P("grid", "member", None),
    )
    return jax.shard_map(local, mesh=mesh, in_specs=in_specs, out_specs=P("member", None, "grid"), check_vma=False)
```
